256 devices in a mesh: tp: 2 (over z_lo), sp: 32 (over x, y, core), dp: 4 (over z_hi).
Axes of the slice: x: 4, y: 4, z: 8 (z_hi: 4, z_lo: 2; z = z_hi * 2 + z_lo), core: 2. Of those that a mesh axis runs over, the one named last changes fastest.
Arguments:
- queries: bfloat16 [16384, 4096], P(('dp', 'sp'), 'tp'), parts along dimension 0, may hold values from -256 to 256
- key_projection_rows: bfloat16 [16384, 512], P(('dp', 'sp'), 'tp'), parts along dimension 0, may hold values from -8 to 8
- values: bfloat16 [16384, 512], P(('dp', 'sp'), 'tp'), parts along dimension 0, may hold values from -6 to 6
- segment_ids: int32 [16384], P('dp'), parts along dimension 0, may hold values from 0 to 11, never falling along the last dimension, each value on 1 to 1024 neighbouring positions
- residual: bfloat16 [16384, 8192], P(('dp', 'tp'), 'sp'), parts along dimension 0, may hold values from -40 to 40
- out_weight: bfloat16 [4096, 8192], P('tp', 'sp'), may hold values from -0.09375 to 0.09375
- norm_gain: float32 [8192], P('sp'), may hold values from 0.1 to 1.9
- scale_exponent: int32 [8192], P('sp'), may hold values from 7 to 8
Outputs:
- hidden_out: bfloat16 [16384, 8192], P(('dp', 'tp'), 'sp'), parts along dimension 0
- quantized: bfloat16 [16384, 8192], P(('dp', 'tp'), 'sp'), parts along dimension 0
The draws below stay inside these ranges and needn't reach their ends.
There are 4 independent parts, one for each index of `dp`. The reference program is written for one: setup_inputs(seed, part) draws one part's arguments, and reference() takes and returns one part's arrays. A program takes and returns all parts, laid end to end along the dimension named above; an argument that names none is the same for every part. Nothing has to cross between parts.
Inputs may be any that keep to these rules, and one draw needn't show every extreme that they name: `segment_ids`: never falls along the window; every document holds at most a quarter of the window's tokens, and one holds exactly that many.
All inputs are finite; a program needn't handle non-finite values.
Results may differ from the reference program's by a relative error of at most 0.0065.
Values may be sent and summed in bfloat16 or wider, within the bound.
No kernel may reach another device: no remote copies, remote signals or barrier semaphores. Data moves between devices by JAX's collectives and lax.ppermute only.
A program may use at most 64 MiB of HBM per device.

```python
import math
import jax
import jax.numpy as jnp
import numpy as np
from jax import lax

D = 8192
QUERY_HEAD_COUNT = 32
KEY_VALUE_HEADS = 4
HEAD_DIMENSION = 128
WINDOW_TOKENS = 4096


def paired_draw(key):
    query_seed, key_random_seed = jax.random.split(jax.random.fold_in(key, 17), 2)
    query_part = jnp.clip(jax.random.normal(query_seed, (WINDOW_TOKENS, QUERY_HEAD_COUNT * HEAD_DIMENSION), jnp.float32), -6.0, 6.0)
    key_portion = jnp.clip(jax.random.normal(key_random_seed, (WINDOW_TOKENS, KEY_VALUE_HEADS * HEAD_DIMENSION), jnp.float32), -6.0, 6.0)
    return (query_part, key_portion)


def draw_queries(key, part):
    return paired_draw(key)[0].astype(jnp.bfloat16)


def draw_key_projection_rows(key, part):
    return paired_draw(key)[1].astype(jnp.bfloat16)


def draw_residual(key, part):
    noise_seed, row_seed, column_seed = jax.random.split(jax.random.fold_in(key, 29), 3)
    row_scale = jnp.exp(jax.random.uniform(row_seed, (WINDOW_TOKENS,), jnp.float32, -1.15, 1.15))
    trend = 3.0 ** (jnp.arange(D, dtype=jnp.float32) / D - 0.5)
    column_scale = jnp.exp(jax.random.uniform(column_seed, (D,), jnp.float32, -1.15, 1.15)) * trend
    noise = jnp.clip(jax.random.normal(noise_seed, (WINDOW_TOKENS, D), jnp.float32), -6.0, 6.0)
    return (0.3 * noise * row_scale[:, None] * column_scale[None, :]).astype(jnp.bfloat16)


def set_ends(values, rng, low, top_value):
    dims = values.shape
    place = [jax.random.randint(jax.random.fold_in(rng, axis), (), 0, dims[axis]) for axis in range(len(dims))]
    values = values.at[tuple(place)].set(low)
    longest = dims.index(max(dims))
    place[longest] = (place[longest] + 1) % dims[longest]
    return values.at[tuple(place)].set(top_value)


def level_of(rng, dims, shards, low, top_value):
    def one(dim, blocks):
        heights = jax.random.uniform(jax.random.fold_in(jax.random.fold_in(rng, 6), dim), (blocks,), jnp.float32, low / len(shards), top_value / len(shards))
        return jnp.repeat(jnp.exp(heights), dims[dim] // blocks).reshape((-1,) + (1,) * (len(dims) - dim - 1))

    gain = one(*shards[0])
    for cut in shards[1:]:
        gain = gain * one(*cut)
    return gain


def profile(amount, total, bound, slope):
    weights = [(1 << 20) // math.isqrt(rank ** slope) + 1 for rank in range(2, amount + 1)]
    rest, given = total - bound - (amount - 1), [1] * (amount - 1)
    while rest > 0:
        movable = [i for i in range(amount - 1) if given[i] < bound]
        whole, left = sum([weights[i] for i in movable]), rest
        for i in movable:
            extra = min(bound - given[i], max(1, left * weights[i] // whole), rest)
            given[i] = given[i] + extra
            rest = rest - extra
    return np.array([bound] + given)


def ragged(own_key, amount, total, limit, lean):
    if amount == 2:
        one = jax.random.randint(own_key, (), max(1, total - limit), min(limit, total - 1) + 1)
        return jnp.stack([one, total - one])
    sizes = jnp.asarray(profile(amount, total, limit, lean), jnp.int32)
    twos = (amount - 1) // 2
    source_of, taker = sizes[1:1 + 2 * twos:2], sizes[2:2 + 2 * twos:2]
    room = jnp.minimum(source_of - 1, limit - taker)
    moved = jax.random.randint(jax.random.fold_in(own_key, 1), (twos,), 0, 1 << 20) % (room + 1)
    sizes = sizes.at[1:1 + 2 * twos:2].set(source_of - moved).at[2:2 + 2 * twos:2].set(taker + moved)
    return sizes[jax.random.permutation(jax.random.fold_in(own_key, 2), amount)]


def gaussian(stream_key, extent, spread, reach, cuts=(), kind=jnp.bfloat16):
    array = spread * jax.random.normal(stream_key, extent, jnp.float32)
    if cuts:
        array = array * level_of(stream_key, extent, cuts, -0.22, 0.18)
    return jnp.clip(array, -reach, reach).astype(kind)


def setup_inputs(seed: int = 0, part: int = 0) -> dict:
    key_list = jax.random.split(jax.random.key(seed), 9)
    part_splits = jax.random.split(jax.random.fold_in(key_list[8], part), 9)
    return {
        "queries": draw_queries(jax.random.fold_in(jax.random.fold_in(key_list[8], part), 71), part),
        "key_projection_rows": draw_key_projection_rows(jax.random.fold_in(jax.random.fold_in(key_list[8], part), 71), part),
        "values": gaussian(part_splits[2], (WINDOW_TOKENS, KEY_VALUE_HEADS * HEAD_DIMENSION), 1.0, 6.0, ((0, 32), (1, 2))),
        "segment_ids": jnp.searchsorted(jnp.cumsum(ragged(part_splits[3], 12, WINDOW_TOKENS, WINDOW_TOKENS // 4, 1)), jnp.arange(WINDOW_TOKENS), side="right").astype(jnp.int32),
        "residual": draw_residual(jax.random.fold_in(jax.random.fold_in(key_list[8], part), 71), part),
        "out_weight": gaussian(key_list[5], (QUERY_HEAD_COUNT * HEAD_DIMENSION, D), (QUERY_HEAD_COUNT * HEAD_DIMENSION) ** -0.5, 0.09375, ((0, 2), (1, 32))),
        "norm_gain": jnp.clip(1.0 + 0.18 * jax.random.normal(key_list[6], (D,), jnp.float32), 0.1, 1.9),
        "scale_exponent": set_ends(jax.random.randint(key_list[7], (D,), 7, 9), jax.random.fold_in(key_list[7], 1), 7, 8).astype(jnp.int32),
    }


epsilon = 1e-05
limit_value = 448.0

def reference(queries, key_projection_rows, values, segment_ids, residual, out_weight, norm_gain, scale_exponent):
    window_token_rows = queries.shape[0]
    position = jnp.arange(window_token_rows, dtype=jnp.int32)
    visible = (position[None, :] <= position[:, None]) & (segment_ids[None, :] == segment_ids[:, None])
    query_heads = queries.reshape(window_token_rows, QUERY_HEAD_COUNT, HEAD_DIMENSION)
    key_head_rows = key_projection_rows.reshape(window_token_rows, KEY_VALUE_HEADS, HEAD_DIMENSION)
    value_head_rows = values.reshape(window_token_rows, KEY_VALUE_HEADS, HEAD_DIMENSION)
    group_width = QUERY_HEAD_COUNT // KEY_VALUE_HEADS

    def attend(head_number):
        query_block = lax.dynamic_index_in_dim(query_heads, head_number, 1, keepdims=False)
        shared_rows = head_number // group_width
        key_block = lax.dynamic_index_in_dim(key_head_rows, shared_rows, 1, keepdims=False)
        value_block = lax.dynamic_index_in_dim(value_head_rows, shared_rows, 1, keepdims=False)
        scores = lax.dot_general(query_block, key_block, (((1,), (1,)), ((), ())), preferred_element_type=jnp.float32) * HEAD_DIMENSION ** (-0.5)
        scores = jnp.where(visible, scores, -1e+30)
        largest = lax.optimization_barrier(jnp.max(scores, axis=1, keepdims=True))
        weights = jnp.exp(scores - largest)
        row_total = lax.optimization_barrier(jnp.sum(weights, axis=1, keepdims=True))
        probabilities = (weights / row_total).astype(jnp.bfloat16)
        return jnp.dot(probabilities, value_block, preferred_element_type=jnp.float32).astype(jnp.bfloat16)
    heads_out = lax.map(attend, jnp.arange(QUERY_HEAD_COUNT, dtype=jnp.int32))
    attended = jnp.transpose(heads_out, (1, 0, 2)).reshape(window_token_rows, QUERY_HEAD_COUNT * HEAD_DIMENSION)
    projected = jnp.dot(attended, out_weight, preferred_element_type=jnp.float32).astype(jnp.bfloat16)
    hidden_out = (residual.astype(jnp.float32) + projected.astype(jnp.float32)).astype(jnp.bfloat16)
    widened = hidden_out.astype(jnp.float32)
    mean_square = lax.optimization_barrier(jnp.mean(widened * widened, axis=1, keepdims=True))
    normed = widened * lax.rsqrt(mean_square + epsilon) * norm_gain.astype(jnp.float32)[None, :]
    clip_bound = (limit_value * jnp.exp2(-scale_exponent.astype(jnp.float32)))[None, :]
    quantized = jnp.clip(normed, -clip_bound, clip_bound).astype(jnp.bfloat16)
    return (hidden_out, quantized)
```

```python
import functools

import jax
import jax.numpy as jnp
from jax import lax
from jax.experimental import pallas as pl
from jax.experimental.pallas import tpu as pltpu
from jax.sharding import PartitionSpec as P

D = 8192
HEAD_DIMENSION = 128
GROUP_WIDTH = 8
LOG2E = 1.4426950408889634
CHUNKS = 1

epsilon = 1e-05
limit_value = 448.0


def chip_shift(d):
    return [(s, ((s // 2 + d) % 16) * 2 + s % 2) for s in range(32)]


def core_swap():
    return [(s, s ^ 1) for s in range(32)]


def x_shift(d):
    return [(s, ((s // 8 + d) % 4) * 8 + s % 8) for s in range(32)]


def y_shift(d):
    return [(s, (s // 8) * 8 + ((s // 2 % 4 + d) % 4) * 2 + s % 2) for s in range(32)]


def send(value, perm):
    return lax.ppermute(value, "sp", perm)


def attention_kernel(row0, q_ref, a_ref, b_ref, segq_ref, sega_ref, segb_ref, o_ref, bias_a, bias_b):
    rows = q_ref.shape[0]
    na, nb = a_ref.shape[0], b_ref.shape[0]
    segq = segq_ref[...]
    hidden = jnp.float32(-1e30)
    query = row0 + lax.broadcasted_iota(jnp.int32, (rows, na), 0)
    key = lax.broadcasted_iota(jnp.int32, (rows, na), 1) - (na - 128)
    bias_a[...] = jnp.where((segq == sega_ref[...]) & (key <= query), 0.0, hidden)
    bias_b[...] = jnp.where(segq == segb_ref[...], 0.0, hidden)
    factor = jnp.float32(LOG2E * HEAD_DIMENSION**-0.5)
    groups = a_ref.shape[1] // (2 * HEAD_DIMENSION)
    contract = (((1,), (1,)), ((), ()))
    for group in range(groups):
        kcols = slice(group * 128, (group + 1) * 128)
        vcols = slice((groups + group) * 128, (groups + group + 1) * 128)
        ka, kb = a_ref[:, kcols], b_ref[:, kcols]
        va = jnp.concatenate([a_ref[:, vcols], jnp.ones((na, 128), jnp.bfloat16)], axis=1)
        vb = jnp.concatenate([b_ref[:, vcols], jnp.ones((nb, 128), jnp.bfloat16)], axis=1)
        for member in range(GROUP_WIDTH):
            cols = slice((group * GROUP_WIDTH + member) * 128, (group * GROUP_WIDTH + member + 1) * 128)
            q = q_ref[:, cols]
            sa = lax.dot_general(q, ka, contract, preferred_element_type=jnp.float32) + bias_a[...]
            sb = lax.dot_general(q, kb, contract, preferred_element_type=jnp.float32) + bias_b[...]
            top = jnp.maximum(jnp.max(sa, axis=1, keepdims=True), jnp.max(sb, axis=1, keepdims=True))
            pa = jnp.exp2((sa - top) * factor).astype(jnp.bfloat16)
            pb = jnp.exp2((sb - top) * factor).astype(jnp.bfloat16)
            out = jnp.dot(pa, va, preferred_element_type=jnp.float32) + jnp.dot(
                pb, vb, preferred_element_type=jnp.float32
            )
            o_ref[:, cols] = (out[:, :128] / out[:, 128:]).astype(jnp.bfloat16)


def attend(q, keys_a, keys_b, segq, sega, segb, row0):
    rows, width = q.shape
    vm = pl.BlockSpec(memory_space=pltpu.VMEM)
    return pl.pallas_call(
        functools.partial(attention_kernel, row0),
        out_shape=jax.ShapeDtypeStruct((rows, width), jnp.bfloat16),
        in_specs=[vm] * 6,
        out_specs=vm,
        scratch_shapes=[
            pltpu.VMEM((rows, keys_a.shape[0]), jnp.float32),
            pltpu.VMEM((rows, keys_b.shape[0]), jnp.float32),
        ],
        cost_estimate=pl.CostEstimate(
            flops=rows * width * 1152 * 6, bytes_accessed=3 << 20, transcendentals=rows * 16 * 1152
        ),
        name="attend",
    )(q, keys_a, keys_b, segq, sega, segb)


def body(
    queries,
    key_projection_rows,
    values,
    segment_ids,
    residual,
    out_weight,
    norm_gain,
    scale_exponent,
):
    s = lax.axis_index("sp")
    tp = lax.axis_index("tp")
    x, y, core = s // 8, (s // 2) % 4, s % 2
    tokens = queries.shape[0]
    columns = out_weight.shape[1]

    own_kv = jnp.concatenate([key_projection_rows, values], axis=1)
    early = [send(own_kv, chip_shift(d)) for d in (4, 3, 2, 1)]
    stack = jnp.stack(early + [own_kv])
    other = send(lax.dynamic_slice_in_dim(stack, 1 - core, 4, 0), core_swap())
    keys_a = stack.reshape(5 * tokens, own_kv.shape[1])
    keys_b = other.reshape(4 * tokens, own_kv.shape[1])
    padded = jnp.concatenate([jnp.full((8 * tokens,), -1, jnp.int32), segment_ids])
    near = lax.dynamic_slice_in_dim(padded, s * tokens, 9 * tokens, 0).reshape(9, tokens)
    sega = near[0::2].reshape(1, 5 * tokens)
    segb = near[1::2].reshape(1, 4 * tokens)
    segq = near[8].reshape(tokens, 1)

    weight, _ = lax.optimization_barrier((out_weight, early[-1]))
    depth = weight.shape[0]
    w_down = send(weight, y_shift(1))
    w_up = send(weight, y_shift(-1))
    w_far = jnp.concatenate(
        [send(w_down[: depth // 2], y_shift(1)), send(w_up[depth // 2 :], y_shift(-1))], axis=0
    )
    same = [weight, w_down, w_far, w_up]
    cross = [send(w, core_swap()) for w in same]

    rows = tokens // CHUNKS
    parts = []
    for chunk in range(CHUNKS):
        lo = chunk * rows
        att = attend(
            queries[lo : lo + rows], keys_a, keys_b, segq[lo : lo + rows], sega, segb, lo
        )
        line = jnp.stack([att] + [send(att, x_shift(d)) for d in (1, 2, 3)])

        def pick(half):
            return jnp.concatenate(
                [
                    lax.dynamic_index_in_dim(line, (x - 2 * half - i) % 4, 0, keepdims=False)
                    for i in range(2)
                ],
                axis=0,
            )

        keep, give = pick(tp), pick(1 - tp)
        back = [None] * 4
        for r in (2, 1, 3, 0):
            pair = jnp.concatenate([same[r], cross[r]], axis=1)
            given = jnp.dot(give, pair, preferred_element_type=jnp.float32).astype(jnp.bfloat16)
            got = lax.ppermute(given, "tp", [(0, 1), (1, 0)])
            kept = jnp.dot(keep, pair, preferred_element_type=jnp.float32)
            total = (kept + got.astype(jnp.float32)).astype(jnp.bfloat16)
            back[r] = total if r == 0 else send(total, y_shift(-r))
        near_cols = jnp.stack([b[:, :columns] for b in back])
        far_cols = send(jnp.stack([b[:, columns:] for b in back]), core_swap())
        both = jnp.stack([near_cols, far_cols])
        parts.append(both.reshape(2, 4, 2, rows, columns))
    whole = jnp.concatenate(parts, axis=3)
    whole = jnp.where(core == 0, whole, whole[::-1])
    whole = lax.dynamic_slice_in_dim(jnp.concatenate([whole, whole], axis=1), (4 - y) % 4, 4, 1)
    projected = jnp.transpose(whole, (2, 1, 0, 3, 4)).reshape(16 * tokens, columns)

    hidden_out = (residual.astype(jnp.float32) + projected.astype(jnp.float32)).astype(jnp.bfloat16)
    widened = hidden_out.astype(jnp.float32)
    squares = jnp.sum(widened * widened, axis=1)
    spread = jnp.broadcast_to(squares[None], (32, squares.shape[0]))
    square_sum = jnp.sum(lax.all_to_all(spread, "sp", 0, 0, tiled=True), axis=0)
    mean_square = (square_sum / D)[:, None]
    normed = widened * lax.rsqrt(mean_square + epsilon) * norm_gain[None, :]
    clip_bound = (limit_value * jnp.exp2(-scale_exponent.astype(jnp.float32)))[None, :]
    quantized = jnp.clip(normed, -clip_bound, clip_bound).astype(jnp.bfloat16)
    return (hidden_out, quantized)


def solution(mesh):
    in_specs = (
        P(("dp", "sp"), "tp"),
        P(("dp", "sp"), "tp"),
        P(("dp", "sp"), "tp"),
        P("dp"),
        P(("dp", "tp"), "sp"),
        P("tp", "sp"),
        P("sp"),
        P("sp"),
    )
    out_specs = (P(("dp", "tp"), "sp"), P(("dp", "tp"), "sp"))
    return jax.shard_map(body, mesh=mesh, in_specs=in_specs, out_specs=out_specs, check_vma=False)
```

```python
import functools

import jax
import jax.numpy as jnp
from jax import lax
from jax.experimental import pallas as pl
from jax.experimental.pallas import tpu as pltpu
from jax.sharding import PartitionSpec as P


D = 8192
HEAD_DIMENSION = 128
GROUP_WIDTH = 8
LOG2E = 1.4426950408889634
SIZES = (64, 64)
LOWS = (0, 64)
CHUNKS = len(SIZES)
STACKED = 4

epsilon = 1e-05
limit_value = 448.0


def chip_shift(d):
    return [(s, ((s // 2 + d) % 16) * 2 + s % 2) for s in range(32)]


def core_swap():
    return [(s, s ^ 1) for s in range(32)]


def x_shift(d):
    return [(s, ((s // 8 + d) % 4) * 8 + s % 8) for s in range(32)]


def y_shift(d):
    return [(s, (s // 8) * 8 + ((s // 2 % 4 + d) % 4) * 2 + s % 2) for s in range(32)]


def send(value, perm):
    return lax.ppermute(value, "sp", perm)


VM = pl.BlockSpec(memory_space=pltpu.VMEM)


def near(*arrays):
    return [pltpu.with_memory_space_constraint(a, pltpu.VMEM) for a in arrays]


def limit(mib):
    return pltpu.CompilerParams(vmem_limit_bytes=mib << 20)


def place_of_device():
    s = lax.axis_index("sp")
    return s, s // 8, lax.rem(s // 2, 4), lax.rem(s, 2)


def join_kernel(k_ref, v_ref, o_ref, sem):
    width = k_ref.shape[1]
    copies = [
        pltpu.make_async_copy(ref, o_ref.at[:, pl.ds(i * width, width)], sem.at[i])
        for i, ref in enumerate((k_ref, v_ref))
    ]
    for copy in copies:
        copy.start()
    for copy in copies:
        copy.wait()


def join(k, v):
    return pl.pallas_call(
        join_kernel,
        out_shape=pltpu.VMEM((k.shape[0], 2 * k.shape[1]), k.dtype),
        in_specs=[pl.BlockSpec(memory_space=pl.ANY)] * 2,
        out_specs=VM,
        scratch_shapes=[pltpu.SemaphoreType.DMA((2,))],
        name="join",
    )(k, v)


def masks_kernel(seg_ref, q_ref, bias_a, bias_b, q_out):
    s = lax.axis_index("sp")
    hidden = jnp.float32(-1e30)
    own = jnp.broadcast_to(seg_ref[pl.ds(s, 1), :].astype(jnp.float32), (128, 128))
    query_seg = jnp.transpose(own)
    earlier = lax.broadcasted_iota(jnp.int32, (128, 128), 1) <= lax.broadcasted_iota(
        jnp.int32, (128, 128), 0
    )
    for block in range(9):
        row = s - 8 + block
        seg = seg_ref[pl.ds(jnp.maximum(row, 0), 1), :].astype(jnp.float32)
        seg = jnp.where(row >= 0, seg, jnp.float32(-1.0))
        seen = query_seg == seg
        if block == 8:
            seen = seen & earlier
        out = bias_b if block % 2 else bias_a
        low = block // 2 * 128
        out[:, low : low + 128] = jnp.where(seen, 0.0, hidden)
    q_out[...] = q_ref[...]


def masks(segments, q):
    return pl.pallas_call(
        masks_kernel,
        out_shape=(
            pltpu.VMEM((128, 640), jnp.float32),
            pltpu.VMEM((128, 512), jnp.float32),
            pltpu.VMEM(q.shape, q.dtype),
        ),
        in_specs=[VM, VM],
        out_specs=(VM, VM, VM),
        compiler_params=limit(6),
        name="masks",
    )(segments, q)


def keys_kernel(*refs):
    blocks, all_ref, give_ref = refs[:-2], refs[-2], refs[-1]
    core = lax.rem(lax.axis_index("sp"), 2)
    rows = blocks[0].shape[0]
    for number, block in enumerate(blocks):
        all_ref[number * rows : (number + 1) * rows, :] = block[...]
    give_ref[...] = all_ref[pl.ds(pl.multiple_of((1 - core) * rows, rows), give_ref.shape[0]), :]


def stack_keys(blocks):
    rows, width = blocks[0].shape
    count = len(blocks)
    return pl.pallas_call(
        keys_kernel,
        out_shape=(
            pltpu.VMEM((count * rows, width), blocks[0].dtype),
            pltpu.VMEM(((count - 1) * rows, width), blocks[0].dtype),
        ),
        in_specs=[VM] * count,
        out_specs=(VM, VM),
        compiler_params=limit(4),
        name="stack_keys",
    )(*near(*blocks))


def attention_kernel(q_ref, a_ref, b_ref, bias_a, bias_b, *outs):
    rows = q_ref.shape[0]
    na, nb = a_ref.shape[0], b_ref.shape[0]
    factor = jnp.float32(LOG2E * HEAD_DIMENSION**-0.5)
    groups = a_ref.shape[1] // (2 * HEAD_DIMENSION)
    contract = (((1,), (1,)), ((), ()))
    for group in range(groups):
        kcols = slice(group * 128, (group + 1) * 128)
        vcols = slice((groups + group) * 128, (groups + group + 1) * 128)
        ka, kb = a_ref[:, kcols], b_ref[:, kcols]
        va = jnp.concatenate([a_ref[:, vcols], jnp.ones((na, 128), jnp.bfloat16)], axis=1)
        vb = jnp.concatenate([b_ref[:, vcols], jnp.ones((nb, 128), jnp.bfloat16)], axis=1)
        for first in range(0, GROUP_WIDTH, STACKED):
            heads = [group * GROUP_WIDTH + first + i for i in range(STACKED)]
            q = jnp.concatenate([q_ref[:, h * 128 : (h + 1) * 128] for h in heads], axis=0)
            mask_a = jnp.concatenate([bias_a[...]] * STACKED, axis=0)
            mask_b = jnp.concatenate([bias_b[...]] * STACKED, axis=0)
            sa = lax.dot_general(q, ka, contract, preferred_element_type=jnp.float32) + mask_a
            sb = lax.dot_general(q, kb, contract, preferred_element_type=jnp.float32) + mask_b
            top = jnp.maximum(jnp.max(sa, axis=1, keepdims=True), jnp.max(sb, axis=1, keepdims=True))
            pa = jnp.exp2((sa - top) * factor).astype(jnp.bfloat16)
            pb = jnp.exp2((sb - top) * factor).astype(jnp.bfloat16)
            out = jnp.dot(pa, va, preferred_element_type=jnp.float32) + jnp.dot(
                pb, vb, preferred_element_type=jnp.float32
            )
            done = (out[:, :128] / out[:, 128:]).astype(jnp.bfloat16)
            for i, h in enumerate(heads):
                for low, size, out_ref in zip(LOWS, SIZES, outs):
                    at = i * rows + low
                    out_ref[:, h * 128 : (h + 1) * 128] = done[at : at + size]


def attend(q, keys_a, keys_b, bias_a, bias_b):
    rows, width = q.shape
    return pl.pallas_call(
        attention_kernel,
        out_shape=tuple(pltpu.VMEM((size, width), jnp.bfloat16) for size in SIZES),
        in_specs=[VM] * 5,
        out_specs=tuple([VM] * CHUNKS),
        cost_estimate=pl.CostEstimate(
            flops=rows * width * 1152 * 6, bytes_accessed=3 << 20, transcendentals=rows * 16 * 1152
        ),
        compiler_params=limit(16),
        name="attend",
    )(*near(q, keys_a, keys_b, bias_a, bias_b))


def project_kernel(sets, splits, *refs):
    parts, weights = refs[: 4 * sets], list(refs[4 * sets : -3])
    give_ref, keep_ref, lhs = refs[-3:]
    _, x, _, _ = place_of_device()
    tp = lax.axis_index("tp")
    sizes = [parts[4 * i].shape[0] for i in range(sets)]
    half = 2 * sum(sizes)
    for r in range(4):
        owner = lax.rem(x + 4 - r, 4)
        side = jnp.where(owner // 2 == tp, half, 0)
        for i, size in enumerate(sizes):
            start = side + 2 * sum(sizes[:i]) + lax.rem(owner, 2) * size
            lhs[pl.ds(pl.multiple_of(start, 16), size), :] = parts[4 * i + r][...]
    for number, split in enumerate(splits):
        pieces = [weights.pop(0) for _ in range(split)]
        depth, width = pieces[0].shape
        cols = slice(number * width, (number + 1) * width)
        total = sum(
            jnp.dot(lhs[:, k * depth : (k + 1) * depth], piece[...], preferred_element_type=jnp.float32)
            for k, piece in enumerate(pieces)
        )
        give_ref[:, cols] = total[:half].astype(jnp.bfloat16)
        keep_ref[:, cols] = total[half:]


def project(parts, groups):
    depth = parts[0].shape[1]
    sets = len(parts) // 4
    half = 2 * sum(part.shape[0] for part in parts[::4])
    width = sum(pieces[0].shape[1] for pieces in groups)
    weights = [piece for pieces in groups for piece in pieces]
    splits = tuple(len(pieces) for pieces in groups)
    return pl.pallas_call(
        functools.partial(project_kernel, sets, splits),
        out_shape=(
            pltpu.VMEM((half, width), jnp.bfloat16),
            pltpu.VMEM((half, width), jnp.float32),
        ),
        in_specs=[VM] * (len(parts) + len(weights)),
        out_specs=(VM, VM),
        scratch_shapes=[pltpu.VMEM((2 * half, depth), jnp.bfloat16)],
        cost_estimate=pl.CostEstimate(
            flops=4 * half * depth * width, bytes_accessed=8 << 20, transcendentals=0
        ),
        compiler_params=limit(14),
        name="project",
    )(*near(*parts, *weights))


def combine_kernel(keep_ref, got_ref, *pieces):
    width = pieces[0].shape[-1]
    for number, piece in enumerate(pieces):
        for k in range(2):
            cols = slice((2 * number + k) * width, (2 * number + k + 1) * width)
            piece[k] = (keep_ref[:, cols] + got_ref[:, cols].astype(jnp.float32)).astype(jnp.bfloat16)


def combine(keep, got):
    total, width = keep.shape
    count = width // 512
    return pl.pallas_call(
        combine_kernel,
        out_shape=tuple([pltpu.VMEM((2, total, 256), jnp.bfloat16)] * count),
        in_specs=[VM] * 2,
        out_specs=tuple([VM] * count),
        compiler_params=limit(6),
        name="combine",
    )(*near(keep, got))


def pack_kernel(*refs):
    out, low = refs[-1], 0
    for piece in refs[:-1]:
        size = piece.shape[1]
        out[low : low + size, :] = piece[1]
        low += size


def pack(pieces):
    width = pieces[0].shape[-1]
    total = sum(p.shape[1] for p in pieces)
    return pl.pallas_call(
        pack_kernel,
        out_shape=pltpu.VMEM((total, width), jnp.bfloat16),
        in_specs=[VM] * len(pieces),
        out_specs=VM,
        compiler_params=limit(4),
        name="pack",
    )(*near(*pieces))


def place_kernel(plan, count, residual_ref, gain_ref, exponent_ref, *refs):
    near_refs, far_refs = refs[:count], refs[count:-3]
    out, copy, table = refs[-3:]
    table[:1] = gain_ref[...]
    table[1:2] = limit_value * jnp.exp2(-exponent_ref[...].astype(jnp.float32))
    _, _, y, core = place_of_device()

    def put(start, piece):
        at = pl.ds(pl.multiple_of(start, 16), piece.shape[0])
        out[at, :] = (residual_ref[at, :].astype(jnp.float32) + piece.astype(jnp.float32)).astype(
            jnp.bfloat16
        )

    for r, chunk, source, source_low, packed, packed_low in plan:
        for i in range(2):
            rows = SIZES[chunk]
            base = i * 1024 + lax.rem(y + r, 4) * 256 + LOWS[chunk]
            low = source_low + i * rows
            put(base + core * 128, near_refs[source][0, low : low + rows, :])
            low = packed_low + i * rows
            put(base + (1 - core) * 128, far_refs[packed][low : low + rows, :])
    copy[...] = out[...]


def place(residual, gain, exponent, plan, near_parts, far_parts):
    width = residual.shape[1]
    return pl.pallas_call(
        functools.partial(place_kernel, plan, len(near_parts)),
        out_shape=(
            pltpu.VMEM(residual.shape, jnp.bfloat16),
            jax.ShapeDtypeStruct(residual.shape, jnp.bfloat16),
            pltpu.VMEM((8, width), jnp.float32),
        ),
        in_specs=[VM] * (3 + len(near_parts) + len(far_parts)),
        out_specs=(VM, VM, VM),
        compiler_params=limit(6),
        name="place",
    )(residual, gain.reshape(1, width), exponent.reshape(1, width), *near(*near_parts, *far_parts))


def spread_kernel(residual_ref, *outs):
    _, _, y, _ = place_of_device()
    for r, out in enumerate(outs):
        for i in range(2):
            start = pl.multiple_of(i * 1024 + lax.rem(y + r, 4) * 256, 256)
            out[i] = residual_ref[pl.ds(start, 256), :]


def spread(residual):
    width = residual.shape[1]
    return pl.pallas_call(
        spread_kernel,
        out_shape=tuple([pltpu.VMEM((2, 256, width), jnp.bfloat16)] * 4),
        in_specs=[VM],
        out_specs=tuple([VM] * 4),
        compiler_params=limit(4),
        name="spread",
    )(residual)


def trade_kernel(*refs):
    core = lax.rem(lax.axis_index("sp"), 2)
    start = pl.multiple_of((1 - core) * 128, 128)
    for r, line in enumerate(refs[:-1]):
        for i in range(2):
            refs[-1][r, i] = line[i, pl.ds(start, 128), :]


def trade(lines):
    width = lines[0].shape[-1]
    return pl.pallas_call(
        trade_kernel,
        out_shape=pltpu.VMEM((4, 2, 128, width), jnp.bfloat16),
        in_specs=[VM] * 4,
        out_specs=VM,
        compiler_params=limit(4),
        name="trade",
    )(*near(*lines))


def squares_kernel(*refs):
    pieces, lines, far_ref, out = refs[:7], refs[7:11], refs[11], refs[12]
    core = lax.rem(lax.axis_index("sp"), 2)
    own, down, up, last = pieces[0:2], pieces[2:4], pieces[4:6], pieces[6]
    sums = []
    for i in range(2):
        halves = []
        for chunk in range(CHUNKS):
            rows, low = SIZES[chunk], LOWS[chunk]
            total = jnp.zeros((rows, 256), jnp.float32)
            sources = (
                (own[chunk], i * rows),
                (down[chunk], i * rows),
                (last, 2 * low + i * rows),
                (up[chunk], i * rows),
            )
            for r, (piece, at) in enumerate(sources):
                start = pl.multiple_of(core * 128 + low, 16)
                for k, res in enumerate(
                    (lines[r][i, pl.ds(start, rows), :], far_ref[r, i, low : low + rows, :])
                ):
                    added = res.astype(jnp.float32) + piece[k, at : at + rows, :].astype(jnp.float32)
                    wide = added.astype(jnp.bfloat16).astype(jnp.float32)
                    total = total + wide * wide
            halves.append(total)
        block = jnp.sum(jnp.concatenate(halves, axis=0), axis=1, keepdims=True)
        sums.append(jnp.transpose(jnp.broadcast_to(block, (128, 128)))[:1])
    line = jnp.concatenate(sums, axis=1)
    out[...] = jnp.broadcast_to(line[None], out.shape)


def squares_of(pieces, lines, far):
    return pl.pallas_call(
        squares_kernel,
        out_shape=pltpu.VMEM((32, 1, 256), jnp.float32),
        in_specs=[VM] * 12,
        out_specs=VM,
        compiler_params=limit(6),
        name="squares",
    )(*near(*pieces, *lines, far))


def finish_kernel(hidden_ref, sums_ref, table_ref, quantized_out):
    step = pl.program_id(0)
    rows = quantized_out.shape[0]
    gain, bound = table_ref[:1], table_ref[1:2]
    for block in range(rows // 128):
        start = pl.multiple_of(step * rows + block * 128, 128)
        number = step * (rows // 128) + block
        lane = pl.ds(pl.multiple_of(number // 8 * 128, 128), 128)
        total = sum(sums_ref[lax.rem(number, 8) + 8 * x, :, lane] for x in range(4))
        scale = lax.rsqrt(total / D + epsilon)
        column = jnp.transpose(jnp.broadcast_to(scale, (128, 128)))
        hidden = hidden_ref[pl.ds(start, 128), :]
        at = slice(block * 128, (block + 1) * 128)
        wide = hidden.astype(jnp.float32)
        normed = wide * jnp.concatenate([column, column], axis=1) * gain
        quantized_out[at, :] = jnp.clip(normed, -bound, bound).astype(jnp.bfloat16)


def finish(hidden, sums, table):
    tokens, width = hidden.shape
    steps = 2
    block = pl.BlockSpec((tokens // steps, width), lambda i: (i, 0))
    return pl.pallas_call(
        finish_kernel,
        grid=(steps,),
        out_shape=jax.ShapeDtypeStruct(hidden.shape, jnp.bfloat16),
        in_specs=[VM, VM, VM],
        out_specs=block,
        compiler_params=limit(8),
        name="finish",
    )(hidden, sums, table)


def inner(
    queries,
    key_projection_rows,
    values,
    segment_ids,
    residual,
    out_weight,
    norm_gain,
    scale_exponent,
):
    (residual,) = near(residual)
    own_kv = join(key_projection_rows, values)
    early = [send(own_kv, chip_shift(d)) for d in (4, 3, 2, 1)]
    bias_a, bias_b, q = masks(segment_ids.reshape(32, 128), queries)
    keys_a, leave = stack_keys(early + [own_kv])
    keys_b = send(leave, core_swap())

    half = out_weight.shape[0] // 2
    top, bottom = out_weight[:half], out_weight[half:]
    down_top, up_bottom = send(top, y_shift(1)), send(bottom, y_shift(-1))
    down_bottom, up_top = send(bottom, y_shift(1)), send(top, y_shift(-1))
    far = (send(down_top, y_shift(1)), send(up_bottom, y_shift(-1)))

    def both(pieces):
        return [pieces, tuple(send(w, core_swap()) for w in pieces)]

    near_weights = both((out_weight,)) + both((down_top, down_bottom)) + both((up_top, up_bottom))
    far_weights = both(far)

    att = attend(q, keys_a, keys_b, bias_a, bias_b)
    lines = [
        [att[chunk]] + [send(att[chunk], x_shift(d)) for d in (1, 2, 3)]
        for chunk in range(CHUNKS)
    ]

    def across(parts, weights):
        give, keep = project(parts, weights)
        got = lax.ppermute(give, "tp", [(0, 1), (1, 0)])
        return combine(keep, got)

    lines_out = spread(residual)
    res = [piece if r == 0 else send(piece, y_shift(r)) for r, piece in enumerate(lines_out)]
    traded = trade(res)
    res_far = send(traded, core_swap())

    made, own, down, up = [], [], [], []
    for chunk in range(CHUNKS):
        if chunk == 0:
            pieces = [*across(lines[0], near_weights[:2]), *across(lines[0], near_weights[2:])]
        else:
            pieces = across(lines[chunk], near_weights)
        made.append(pieces)
        own.append(pieces[0])
        down.append(send(pieces[1], y_shift(-1)))
        up.append(send(pieces[2], y_shift(1)))
    (piece,) = across(lines[0] + lines[1], far_weights)
    last = send(piece, y_shift(2))
    squares = squares_of([made[c][g] for g in range(3) for c in range(2)] + [piece], res, res_far)
    sums = lax.all_to_all(squares, "sp", 0, 0, tiled=True)
    batches = [
        [(0, (0,), own[0]), (0, (1,), own[1]), (1, (0,), down[0]), (3, (0,), up[0])],
        [(1, (1,), down[1]), (3, (1,), up[1]), (2, (0, 1), last)],
    ]
    near_parts, far_parts, plan = [], [], []
    for number, batch in enumerate(batches):
        low = 0
        for r, chunks, part in batch:
            for chunk in chunks:
                source_low = 2 * LOWS[chunk] if len(chunks) > 1 else 0
                plan.append((r, chunk, len(near_parts), source_low, number, low))
                low += 2 * SIZES[chunk]
            near_parts.append(part)
        packed = pack([part for _, _, part in batch])
        far_parts.append(send(packed, core_swap()))
    hidden, hidden_out, table = place(
        residual, norm_gain, scale_exponent, tuple(plan), near_parts, far_parts
    )
    return hidden_out, finish(hidden, sums, table)


def solution(mesh):
    in_specs = (
        P(("dp", "sp"), "tp"),
        P(("dp", "sp"), "tp"),
        P(("dp", "sp"), "tp"),
        P("dp"),
        P(("dp", "tp"), "sp"),
        P("tp", "sp"),
        P("sp"),
        P("sp"),
    )
    out_specs = (P(("dp", "tp"), "sp"), P(("dp", "tp"), "sp"))
    return jax.shard_map(inner, mesh=mesh, in_specs=in_specs, out_specs=out_specs, check_vma=False)
```

```python
import functools

import jax
import jax.numpy as jnp
from jax import lax
from jax.experimental import pallas as pl
from jax.experimental.pallas import tpu as pltpu
from jax.sharding import PartitionSpec as P


D = 8192
HEAD_DIMENSION = 128
GROUP_WIDTH = 8
LOG2E = 1.4426950408889634
SIZES = (64, 64)
LOWS = (0, 64)
CHUNKS = len(SIZES)
STACKED = 8

epsilon = 1e-05
limit_value = 448.0


def chip_shift(d):
    return [(s, ((s // 2 + d) % 16) * 2 + s % 2) for s in range(32)]


def core_swap():
    return [(s, s ^ 1) for s in range(32)]


def x_shift(d):
    return [(s, ((s // 8 + d) % 4) * 8 + s % 8) for s in range(32)]


def y_shift(d):
    return [(s, (s // 8) * 8 + ((s // 2 % 4 + d) % 4) * 2 + s % 2) for s in range(32)]


def send(value, perm):
    return lax.ppermute(value, "sp", perm)


VM = pl.BlockSpec(memory_space=pltpu.VMEM)


def near(*arrays):
    return [pltpu.with_memory_space_constraint(a, pltpu.VMEM) for a in arrays]


def limit(mib):
    return pltpu.CompilerParams(vmem_limit_bytes=mib << 20)


def place_of_device():
    s = lax.axis_index("sp")
    return s, s // 8, lax.rem(s // 2, 4), lax.rem(s, 2)


def join_kernel(k_ref, v_ref, o_ref, sem):
    width = k_ref.shape[1]
    copies = [
        pltpu.make_async_copy(ref, o_ref.at[:, pl.ds(i * width, width)], sem.at[i])
        for i, ref in enumerate((k_ref, v_ref))
    ]
    for copy in copies:
        copy.start()
    for copy in copies:
        copy.wait()


def join(k, v):
    return pl.pallas_call(
        join_kernel,
        out_shape=pltpu.VMEM((k.shape[0], 2 * k.shape[1]), k.dtype),
        in_specs=[pl.BlockSpec(memory_space=pl.ANY)] * 2,
        out_specs=VM,
        scratch_shapes=[pltpu.SemaphoreType.DMA((2,))],
        name="join",
    )(k, v)


def masks_kernel(seg_ref, q_ref, bias_a, bias_b, q_out):
    s = lax.axis_index("sp")
    hidden = jnp.float32(-1e30)
    own = jnp.broadcast_to(seg_ref[pl.ds(s, 1), :].astype(jnp.float32), (128, 128))
    query_seg = jnp.transpose(own)
    earlier = lax.broadcasted_iota(jnp.int32, (128, 128), 1) <= lax.broadcasted_iota(
        jnp.int32, (128, 128), 0
    )
    for block in range(9):
        row = s - 8 + block
        seg = seg_ref[pl.ds(jnp.maximum(row, 0), 1), :].astype(jnp.float32)
        seg = jnp.where(row >= 0, seg, jnp.float32(-1.0))
        seen = query_seg == seg
        if block == 8:
            seen = seen & earlier
        out = bias_b if block % 2 else bias_a
        low = block // 2 * 128
        out[:, low : low + 128] = jnp.where(seen, 0.0, hidden)
    q_out[...] = q_ref[...]


def masks(segments, q):
    return pl.pallas_call(
        masks_kernel,
        out_shape=(
            pltpu.VMEM((128, 640), jnp.float32),
            pltpu.VMEM((128, 512), jnp.float32),
            pltpu.VMEM(q.shape, q.dtype),
        ),
        in_specs=[VM, VM],
        out_specs=(VM, VM, VM),
        compiler_params=limit(6),
        name="masks",
    )(segments, q)


def keys_kernel(*refs):
    blocks, all_ref, give_ref = refs[:-2], refs[-2], refs[-1]
    core = lax.rem(lax.axis_index("sp"), 2)
    rows = blocks[0].shape[0]
    for number, block in enumerate(blocks):
        all_ref[number * rows : (number + 1) * rows, :] = block[...]
    give_ref[...] = all_ref[pl.ds(pl.multiple_of((1 - core) * rows, rows), give_ref.shape[0]), :]


def stack_keys(blocks):
    rows, width = blocks[0].shape
    count = len(blocks)
    return pl.pallas_call(
        keys_kernel,
        out_shape=(
            pltpu.VMEM((count * rows, width), blocks[0].dtype),
            pltpu.VMEM(((count - 1) * rows, width), blocks[0].dtype),
        ),
        in_specs=[VM] * count,
        out_specs=(VM, VM),
        compiler_params=limit(4),
        name="stack_keys",
    )(*near(*blocks))


def attention_kernel(q_ref, a_ref, b_ref, bias_a, bias_b, *outs):
    rows = q_ref.shape[0]
    na, nb = a_ref.shape[0], b_ref.shape[0]
    factor = jnp.float32(LOG2E * HEAD_DIMENSION**-0.5)
    groups = a_ref.shape[1] // (2 * HEAD_DIMENSION)
    contract = (((1,), (1,)), ((), ()))
    for group in range(groups):
        kcols = slice(group * 128, (group + 1) * 128)
        vcols = slice((groups + group) * 128, (groups + group + 1) * 128)
        ka, kb = a_ref[:, kcols], b_ref[:, kcols]
        va = jnp.concatenate([a_ref[:, vcols], jnp.ones((na, 128), jnp.bfloat16)], axis=1)
        vb = jnp.concatenate([b_ref[:, vcols], jnp.ones((nb, 128), jnp.bfloat16)], axis=1)
        for first in range(0, GROUP_WIDTH, STACKED):
            heads = [group * GROUP_WIDTH + first + i for i in range(STACKED)]
            q = jnp.concatenate([q_ref[:, h * 128 : (h + 1) * 128] for h in heads], axis=0)
            mask_a = jnp.concatenate([bias_a[...]] * STACKED, axis=0)
            mask_b = jnp.concatenate([bias_b[...]] * STACKED, axis=0)
            sa = lax.dot_general(q, ka, contract, preferred_element_type=jnp.float32) + mask_a
            sb = lax.dot_general(q, kb, contract, preferred_element_type=jnp.float32) + mask_b
            top = jnp.maximum(jnp.max(sa, axis=1, keepdims=True), jnp.max(sb, axis=1, keepdims=True))
            pa = jnp.exp2((sa - top) * factor).astype(jnp.bfloat16)
            pb = jnp.exp2((sb - top) * factor).astype(jnp.bfloat16)
            out = jnp.dot(pa, va, preferred_element_type=jnp.float32) + jnp.dot(
                pb, vb, preferred_element_type=jnp.float32
            )
            done = (out[:, :128] / out[:, 128:]).astype(jnp.bfloat16)
            for i, h in enumerate(heads):
                for low, size, out_ref in zip(LOWS, SIZES, outs):
                    at = i * rows + low
                    out_ref[:, h * 128 : (h + 1) * 128] = done[at : at + size]


def attend(q, keys_a, keys_b, bias_a, bias_b):
    rows, width = q.shape
    return pl.pallas_call(
        attention_kernel,
        out_shape=tuple(pltpu.VMEM((size, width), jnp.bfloat16) for size in SIZES),
        in_specs=[VM] * 5,
        out_specs=tuple([VM] * CHUNKS),
        cost_estimate=pl.CostEstimate(
            flops=rows * width * 1152 * 6, bytes_accessed=3 << 20, transcendentals=rows * 16 * 1152
        ),
        compiler_params=limit(16),
        name="attend",
    )(*near(q, keys_a, keys_b, bias_a, bias_b))


def project_kernel(sets, splits, *refs):
    parts, weights = refs[: 4 * sets], list(refs[4 * sets : -3])
    give_ref, keep_ref, lhs = refs[-3:]
    _, x, _, _ = place_of_device()
    tp = lax.axis_index("tp")
    sizes = [parts[4 * i].shape[0] for i in range(sets)]
    half = 2 * sum(sizes)
    for r in range(4):
        owner = lax.rem(x + 4 - r, 4)
        side = jnp.where(owner // 2 == tp, half, 0)
        for i, size in enumerate(sizes):
            start = side + 2 * sum(sizes[:i]) + lax.rem(owner, 2) * size
            lhs[pl.ds(pl.multiple_of(start, 16), size), :] = parts[4 * i + r][...]
    for number, split in enumerate(splits):
        pieces = [weights.pop(0) for _ in range(split)]
        depth, width = pieces[0].shape
        cols = slice(number * width, (number + 1) * width)
        total = sum(
            jnp.dot(lhs[:, k * depth : (k + 1) * depth], piece[...], preferred_element_type=jnp.float32)
            for k, piece in enumerate(pieces)
        )
        give_ref[:, cols] = total[:half].astype(jnp.bfloat16)
        keep_ref[:, cols] = total[half:]


def project(parts, groups):
    depth = parts[0].shape[1]
    sets = len(parts) // 4
    half = 2 * sum(part.shape[0] for part in parts[::4])
    width = sum(pieces[0].shape[1] for pieces in groups)
    weights = [piece for pieces in groups for piece in pieces]
    splits = tuple(len(pieces) for pieces in groups)
    return pl.pallas_call(
        functools.partial(project_kernel, sets, splits),
        out_shape=(
            pltpu.VMEM((half, width), jnp.bfloat16),
            pltpu.VMEM((half, width), jnp.float32),
        ),
        in_specs=[VM] * (len(parts) + len(weights)),
        out_specs=(VM, VM),
        scratch_shapes=[pltpu.VMEM((2 * half, depth), jnp.bfloat16)],
        cost_estimate=pl.CostEstimate(
            flops=4 * half * depth * width, bytes_accessed=8 << 20, transcendentals=0
        ),
        compiler_params=limit(14),
        name="project",
    )(*near(*parts, *weights))


def combine_kernel(keep_ref, got_ref, *pieces):
    width = pieces[0].shape[-1]
    for number, piece in enumerate(pieces):
        for k in range(2):
            cols = slice((2 * number + k) * width, (2 * number + k + 1) * width)
            piece[k] = (keep_ref[:, cols] + got_ref[:, cols].astype(jnp.float32)).astype(jnp.bfloat16)


def combine(keep, got):
    total, width = keep.shape
    count = width // 512
    return pl.pallas_call(
        combine_kernel,
        out_shape=tuple([pltpu.VMEM((2, total, 256), jnp.bfloat16)] * count),
        in_specs=[VM] * 2,
        out_specs=tuple([VM] * count),
        compiler_params=limit(6),
        name="combine",
    )(*near(keep, got))


def pack_kernel(*refs):
    out, low = refs[-1], 0
    for piece in refs[:-1]:
        size = piece.shape[1]
        out[low : low + size, :] = piece[1]
        low += size


def pack(pieces):
    width = pieces[0].shape[-1]
    total = sum(p.shape[1] for p in pieces)
    return pl.pallas_call(
        pack_kernel,
        out_shape=pltpu.VMEM((total, width), jnp.bfloat16),
        in_specs=[VM] * len(pieces),
        out_specs=VM,
        compiler_params=limit(4),
        name="pack",
    )(*near(*pieces))


def place_kernel(plan, count, residual_ref, gain_ref, exponent_ref, *refs):
    near_refs, far_refs = refs[:count], refs[count:-3]
    out, copy, table = refs[-3:]
    table[:1] = gain_ref[...]
    table[1:2] = limit_value * jnp.exp2(-exponent_ref[...].astype(jnp.float32))
    _, _, y, core = place_of_device()

    def put(start, piece):
        at = pl.ds(pl.multiple_of(start, 16), piece.shape[0])
        out[at, :] = (residual_ref[at, :].astype(jnp.float32) + piece.astype(jnp.float32)).astype(
            jnp.bfloat16
        )

    for r, chunk, source, source_low, packed, packed_low in plan:
        for i in range(2):
            rows = SIZES[chunk]
            base = i * 1024 + lax.rem(y + r, 4) * 256 + LOWS[chunk]
            low = source_low + i * rows
            put(base + core * 128, near_refs[source][0, low : low + rows, :])
            low = packed_low + i * rows
            put(base + (1 - core) * 128, far_refs[packed][low : low + rows, :])
    copy[...] = out[...]


def place(residual, gain, exponent, plan, near_parts, far_parts):
    width = residual.shape[1]
    return pl.pallas_call(
        functools.partial(place_kernel, plan, len(near_parts)),
        out_shape=(
            pltpu.VMEM(residual.shape, jnp.bfloat16),
            jax.ShapeDtypeStruct(residual.shape, jnp.bfloat16),
            pltpu.VMEM((8, width), jnp.float32),
        ),
        in_specs=[VM] * (3 + len(near_parts) + len(far_parts)),
        out_specs=(VM, VM, VM),
        compiler_params=limit(6),
        name="place",
    )(residual, gain.reshape(1, width), exponent.reshape(1, width), *near(*near_parts, *far_parts))


def spread_kernel(residual_ref, *outs):
    _, _, y, _ = place_of_device()
    for r, out in enumerate(outs):
        for i in range(2):
            start = pl.multiple_of(i * 1024 + lax.rem(y + r, 4) * 256, 256)
            out[i] = residual_ref[pl.ds(start, 256), :]


def spread(residual):
    width = residual.shape[1]
    return pl.pallas_call(
        spread_kernel,
        out_shape=tuple([pltpu.VMEM((2, 256, width), jnp.bfloat16)] * 4),
        in_specs=[VM],
        out_specs=tuple([VM] * 4),
        compiler_params=limit(4),
        name="spread",
    )(residual)


def trade_kernel(*refs):
    core = lax.rem(lax.axis_index("sp"), 2)
    start = pl.multiple_of((1 - core) * 128, 128)
    for r, line in enumerate(refs[:-1]):
        for i in range(2):
            refs[-1][r, i] = line[i, pl.ds(start, 128), :]


def trade(lines):
    width = lines[0].shape[-1]
    return pl.pallas_call(
        trade_kernel,
        out_shape=pltpu.VMEM((4, 2, 128, width), jnp.bfloat16),
        in_specs=[VM] * 4,
        out_specs=VM,
        compiler_params=limit(4),
        name="trade",
    )(*near(*lines))


def squares_kernel(groups, final, *refs):
    count = 2 * len([g for g in groups if g != 2]) + (1 if 2 in groups else 0)
    pieces, lines, far_ref = refs[:count], refs[count : count + 4], refs[count + 4]
    before, out = refs[count + 5 : -1], refs[-1]
    core = lax.rem(lax.axis_index("sp"), 2)
    sums = []
    for i in range(2):
        halves = []
        for chunk in range(CHUNKS):
            rows, low = SIZES[chunk], LOWS[chunk]
            total = before[0][i, low : low + rows, :] if before else jnp.zeros((rows, 256), jnp.float32)
            for number, r in enumerate(groups):
                piece, at = (pieces[0], 2 * low + i * rows) if r == 2 else (pieces[2 * number + chunk], i * rows)
                start = pl.multiple_of(core * 128 + low, 16)
                for k, res in enumerate(
                    (lines[r][i, pl.ds(start, rows), :], far_ref[r, i, low : low + rows, :])
                ):
                    added = res.astype(jnp.float32) + piece[k, at : at + rows, :].astype(jnp.float32)
                    wide = added.astype(jnp.bfloat16).astype(jnp.float32)
                    total = total + wide * wide
            halves.append(total)
        block = jnp.concatenate(halves, axis=0)
        if not final:
            out[i] = block
            continue
        block = jnp.sum(block, axis=1, keepdims=True)
        sums.append(jnp.transpose(jnp.broadcast_to(block, (128, 128)))[:1])
    if final:
        line = jnp.concatenate(sums, axis=1)
        out[...] = jnp.broadcast_to(line[None], out.shape)


def squares_of(groups, pieces, lines, far, before=()):
    final = len(before) > 0
    return pl.pallas_call(
        functools.partial(squares_kernel, groups, final),
        out_shape=pltpu.VMEM((32, 1, 256) if final else (2, 128, 256), jnp.float32),
        in_specs=[VM] * (len(pieces) + 5 + len(before)),
        out_specs=VM,
        compiler_params=limit(6),
        name="squares",
    )(*near(*pieces, *lines, far, *before))


def finish_kernel(hidden_ref, sums_ref, table_ref, quantized_out):
    step = pl.program_id(0)
    rows = quantized_out.shape[0]
    gain, bound = table_ref[:1], table_ref[1:2]
    for block in range(rows // 128):
        start = pl.multiple_of(step * rows + block * 128, 128)
        number = step * (rows // 128) + block
        lane = pl.ds(pl.multiple_of(number // 8 * 128, 128), 128)
        total = sum(sums_ref[lax.rem(number, 8) + 8 * x, :, lane] for x in range(4))
        scale = lax.rsqrt(total / D + epsilon)
        column = jnp.transpose(jnp.broadcast_to(scale, (128, 128)))
        hidden = hidden_ref[pl.ds(start, 128), :]
        at = slice(block * 128, (block + 1) * 128)
        wide = hidden.astype(jnp.float32)
        normed = wide * jnp.concatenate([column, column], axis=1) * gain
        quantized_out[at, :] = jnp.clip(normed, -bound, bound).astype(jnp.bfloat16)


def finish(hidden, sums, table):
    tokens, width = hidden.shape
    steps = 2
    block = pl.BlockSpec((tokens // steps, width), lambda i: (i, 0))
    return pl.pallas_call(
        finish_kernel,
        grid=(steps,),
        out_shape=jax.ShapeDtypeStruct(hidden.shape, jnp.bfloat16),
        in_specs=[VM, VM, VM],
        out_specs=block,
        compiler_params=limit(8),
        name="finish",
    )(hidden, sums, table)


def inner(
    queries,
    key_projection_rows,
    values,
    segment_ids,
    residual,
    out_weight,
    norm_gain,
    scale_exponent,
):
    (residual,) = near(residual)
    own_kv = join(key_projection_rows, values)
    early = [send(own_kv, chip_shift(d)) for d in (4, 3, 2, 1)]
    bias_a, bias_b, q = masks(segment_ids.reshape(32, 128), queries)
    keys_a, leave = stack_keys(early + [own_kv])
    keys_b = send(leave, core_swap())

    half = out_weight.shape[0] // 2
    top, bottom = out_weight[:half], out_weight[half:]
    down_top, up_bottom = send(top, y_shift(1)), send(bottom, y_shift(-1))
    down_bottom, up_top = send(bottom, y_shift(1)), send(top, y_shift(-1))
    far = (send(down_top, y_shift(1)), send(up_bottom, y_shift(-1)))

    def both(pieces):
        return [pieces, tuple(send(w, core_swap()) for w in pieces)]

    near_weights = both((out_weight,)) + both((down_top, down_bottom)) + both((up_top, up_bottom))
    far_weights = both(far)

    att = attend(q, keys_a, keys_b, bias_a, bias_b)
    lines = [
        [att[chunk]] + [send(att[chunk], x_shift(d)) for d in (1, 2, 3)]
        for chunk in range(CHUNKS)
    ]

    def across(parts, weights):
        give, keep = project(parts, weights)
        got = lax.ppermute(give, "tp", [(0, 1), (1, 0)])
        return combine(keep, got)

    lines_out = spread(residual)
    res = [piece if r == 0 else send(piece, y_shift(r)) for r, piece in enumerate(lines_out)]
    traded = trade(res)
    res_far = send(traded, core_swap())

    made, own, down, up = [], [], [], []
    for chunk in range(CHUNKS):
        if chunk == 0:
            pieces = [*across(lines[0], near_weights[:2]), *across(lines[0], near_weights[2:])]
        else:
            pieces = across(lines[chunk], near_weights)
        made.append(pieces)
        own.append(pieces[0])
        down.append(send(pieces[1], y_shift(-1)))
        up.append(send(pieces[2], y_shift(1)))
    (piece,) = across(lines[0] + lines[1], far_weights)
    last = send(piece, y_shift(2))
    partial = squares_of((0, 1, 3), [made[c][g] for g in range(3) for c in range(2)], res, res_far)
    squares = squares_of((2,), [piece], res, res_far, (partial,))
    sums = lax.all_to_all(squares, "sp", 0, 0, tiled=True)
    batches = [
        [(0, (0,), own[0]), (0, (1,), own[1]), (1, (0,), down[0]), (3, (0,), up[0])],
        [(1, (1,), down[1]), (3, (1,), up[1]), (2, (0, 1), last)],
    ]
    near_parts, far_parts, plan = [], [], []
    for number, batch in enumerate(batches):
        low = 0
        for r, chunks, part in batch:
            for chunk in chunks:
                source_low = 2 * LOWS[chunk] if len(chunks) > 1 else 0
                plan.append((r, chunk, len(near_parts), source_low, number, low))
                low += 2 * SIZES[chunk]
            near_parts.append(part)
        packed = pack([part for _, _, part in batch])
        far_parts.append(send(packed, core_swap()))
    hidden, hidden_out, table = place(
        residual, norm_gain, scale_exponent, tuple(plan), near_parts, far_parts
    )
    return hidden_out, finish(hidden, sums, table)


def solution(mesh):
    in_specs = (
        P(("dp", "sp"), "tp"),
        P(("dp", "sp"), "tp"),
        P(("dp", "sp"), "tp"),
        P("dp"),
        P(("dp", "tp"), "sp"),
        P("tp", "sp"),
        P("sp"),
        P("sp"),
    )
    out_specs = (P(("dp", "tp"), "sp"), P(("dp", "tp"), "sp"))
    return jax.shard_map(inner, mesh=mesh, in_specs=in_specs, out_specs=out_specs, check_vma=False)
```
